32 devices in a mesh: groups: 2 (over y), ctx: 4 (over z), head: 2 (over x), sub: 2 (over core).
Axes of the slice: x: 2, y: 2, z: 4, core: 2. Of those that a mesh axis runs over, the one named last changes fastest.
Arguments:
- queries: float32 [2048, 4096], P(('groups', 'ctx', 'sub'), 'head'), parts along dimension 0, may hold values from -6 to 6
- key_vectors: float32 [2048, 4096], P(('groups', 'ctx', 'sub'), 'head'), parts along dimension 0, may hold values from -6 to 6
- value_vectors: float32 [2048, 4096], P(('groups', 'ctx', 'sub'), 'head'), parts along dimension 0, may hold values from -6 to 6
- damping: float32 [4096], P('head'), may hold values from 0.25 to 4
- grad_output: float32 [2048, 4096], P(('groups', 'ctx', 'sub'), 'head'), parts along dimension 0, may hold values from -6 to 6
Outputs:
- mixed_out: float32 [2048, 4096], P(('groups', 'ctx', 'sub'), 'head'), parts along dimension 0
- grad_queries: float32 [2048, 4096], P(('groups', 'ctx', 'sub'), 'head'), parts along dimension 0
- grad_keys: float32 [2048, 4096], P(('groups', 'ctx', 'sub'), 'head'), parts along dimension 0
- grad_values: float32 [2048, 4096], P(('groups', 'ctx', 'sub'), 'head'), parts along dimension 0
The draws below stay inside these ranges and needn't reach their ends.
There are 2 independent parts, one for each index of `groups`. The reference program is written for one: setup_inputs(seed, part) draws one part's arguments, and reference() takes and returns one part's arrays. A program takes and returns all parts, laid end to end along the dimension named above; an argument that names none is the same for every part. Nothing has to cross between parts.
All inputs are finite; a program needn't handle non-finite values.
Results may differ from the reference program's by a relative error of at most 0.0003.
Values sent between devices are 32-bit elements; how exact they have to be, the bound alone decides.
No kernel may reach another device: no remote copies, remote signals or barrier semaphores. Data moves between devices by JAX's collectives and lax.ppermute only.
A program may use at most 128 MiB of HBM per device.

```python
import math
import jax
import jax.numpy as jnp
from jax import lax

HEADS = 32
DK = 128
ITERS = 3
TOK_DEV = 128
TOKENS = 1024


def draw_key_vectors(key, part):
    column_scale = jnp.exp(jax.random.uniform(jax.random.fold_in(key, 1), (HEADS * DK,), jnp.float32, math.log(0.3), math.log(3.0)))
    base = jnp.clip(jax.random.normal(jax.random.fold_in(key, 2), (TOKENS, HEADS * DK), jnp.float32), -6.0, 6.0)
    return (base * column_scale * DK ** (-0.5)).astype(jnp.float32)


def steps_of(stream_key, dims, pieces, least, largest):
    level = 1.0
    for axis_at, shards_of in pieces:
        steps = jax.random.uniform(jax.random.fold_in(jax.random.fold_in(stream_key, 6), axis_at), (shards_of,), jnp.float32, least / len(pieces), largest / len(pieces))
        level = level * jnp.repeat(jnp.exp(steps), dims[axis_at] // shards_of).reshape((-1,) + (1,) * (len(dims) - 1 - axis_at))
    return level


def normal_values(rng, shape, deviation, bound, shards=(), kind=jnp.bfloat16):
    drawn = jax.random.normal(rng, shape, jnp.float32) * deviation
    if len(shards) > 0:
        drawn = steps_of(rng, shape, shards, -0.22, 0.18) * drawn
    return jnp.clip(drawn, min=-bound, max=bound).astype(kind)


def setup_inputs(seed: int = 0, part: int = 0) -> dict:
    arg_keys = jax.random.split(jax.random.key(seed), 6)
    part_keys = jax.random.split(jax.random.fold_in(arg_keys[5], part), 6)
    queries = normal_values(part_keys[0], (TOKENS, HEADS * DK), 1.0, 6.0, ((0, 8), (1, 2)), jnp.float32)
    key_vectors = draw_key_vectors(jax.random.fold_in(jax.random.fold_in(arg_keys[5], part), 71), part)
    value_vectors = normal_values(part_keys[2], (TOKENS, HEADS * DK), 1.0, 6.0, ((0, 8), (1, 2)), jnp.float32)
    damping = jnp.clip(jnp.exp(math.log(4.0) - 2.7725887 * jax.random.uniform(arg_keys[3], (HEADS * DK,), jnp.float32) ** steps_of(arg_keys[3], (HEADS * DK,), ((0, 2),), -0.2, 0.2)), 0.25, 4.0)
    grad_output = normal_values(part_keys[4], (TOKENS, HEADS * DK), 1.0, 6.0, ((0, 8), (1, 2)), jnp.float32)
    return {"queries": queries, "key_vectors": key_vectors, "value_vectors": value_vectors, "damping": damping, "grad_output": grad_output}


highest = lax.Precision.HIGHEST

def causal_table(row_count):
    positions = jnp.arange(row_count, dtype=jnp.int32)
    return (positions[None, :] <= positions[:, None]).astype(jnp.float32)

def apply_system(direction, key_heads, damp, kk_prior, causal):
    prior_part = jnp.einsum('hde,hre->hrd', kk_prior, direction, precision=highest)
    scores = jnp.einsum('hre,hse->hrs', direction, key_heads, precision=highest) * causal
    local_part = jnp.einsum('hrs,hsd->hrd', scores, key_heads, precision=highest)
    return damp * direction + prior_part + local_part

def block_output(query_heads, key_heads, value_heads, damp, kk_prior, vk_prior):
    causal = causal_table(query_heads.shape[1])
    solved = jnp.zeros_like(query_heads)
    resid = query_heads
    direction = query_heads
    resid_sq = lax.optimization_barrier(jnp.sum(resid * resid, axis=-1, keepdims=True))
    for iteration in range(ITERS):
        image = apply_system(direction, key_heads, damp, kk_prior, causal)
        step_size = resid_sq / lax.optimization_barrier(jnp.sum(direction * image, axis=-1, keepdims=True))
        solved = solved + step_size * direction
        resid = resid - step_size * image
        next_sq = lax.optimization_barrier(jnp.sum(resid * resid, axis=-1, keepdims=True))
        direction = resid + next_sq / resid_sq * direction
        resid_sq = next_sq
    prior_part = jnp.einsum('hve,hre->hrv', vk_prior, solved, precision=highest)
    scores = jnp.einsum('hre,hse->hrs', solved, key_heads, precision=highest) * causal
    return prior_part + jnp.einsum('hrs,hsv->hrv', scores, value_heads, precision=highest)

def block_sums(key_heads, value_heads):
    key_key = jnp.einsum('hrd,hre->hde', key_heads, key_heads, precision=highest)
    value_key = jnp.einsum('hrv,hre->hve', value_heads, key_heads, precision=highest)
    return (key_key, value_key)

def reference(queries, key_vectors, value_vectors, damping, grad_output):
    span_count = TOKENS // TOK_DEV

    def to_blocks(values):
        return values.reshape(span_count, TOK_DEV, HEADS, DK).transpose(0, 2, 1, 3)

    def from_blocks(values):
        return values.transpose(0, 2, 1, 3).reshape(TOKENS, HEADS * DK)
    damp = damping.reshape(HEADS, 1, DK)

    def whole(query_all, key_all, value_all):

        def advance(carry, block):
            kk_prior, vk_prior = carry
            query_block, key_block, value_block = block
            output = block_output(query_block, key_block, value_block, damp, kk_prior, vk_prior)
            kk_added, vk_added = block_sums(key_block, value_block)
            return ((kk_prior + kk_added, vk_prior + vk_added), output)
        zero_state = jnp.zeros((HEADS, DK, DK), jnp.float32)
        blocks = (to_blocks(query_all), to_blocks(key_all), to_blocks(value_all))
        final_state, outputs = lax.scan(jax.checkpoint(advance), (zero_state, zero_state), blocks)
        return from_blocks(outputs)
    mixed_out, pullback = jax.vjp(whole, queries, key_vectors, value_vectors)
    grad_queries, grad_keys, grad_values = pullback(grad_output)
    return (mixed_out, grad_queries, grad_keys, grad_values)
```

```python
import functools

import jax
import jax.numpy as jnp
from jax import lax
from jax.experimental import pallas as pl
from jax.experimental.pallas import tpu as pltpu
from jax.sharding import PartitionSpec as P

DK = 128
ROW_DIAG, ROW_VK, ROWS = DK, DK + 8, 3 * DK + 8
VMEM_BYTES = 48 * 1024 * 1024

f32, bf16 = jnp.float32, jnp.bfloat16


def split(x):
    high = x.astype(bf16)
    return high, (x - high.astype(f32)).astype(bf16)


def each(fn, *lists):
    return [fn(*items) for items in zip(*lists)]


def beside(*parts):
    return tuple(jnp.concatenate(half, axis=1) for half in zip(*parts))


def above(*parts):
    return tuple(jnp.concatenate(half, axis=0) for half in zip(*parts))


def dot(a, b, rhs_dim):
    return lax.dot_general(a, b, (((1,), (rhs_dim,)), ((), ())), preferred_element_type=f32)


def mm(a, b):
    return dot(a[0], b[0], 0) + (dot(a[0], b[1], 0) + dot(a[1], b[0], 0))


def mm_t(a, b):
    return dot(a[0], b[0], 1) + (dot(a[0], b[1], 1) + dot(a[1], b[0], 1))


def positions():
    row = lax.broadcasted_iota(jnp.int32, (DK, DK), 0)
    return row, lax.broadcasted_iota(jnp.int32, (DK, DK), 1)


def pack_into(ref, at, first, second, vk_first, vk_second):
    row, col = positions()
    ref[at, 0:DK, :] = jnp.where(row > col, first, second)
    diagonal = jnp.sum(jnp.where(row == col, first, 0.0), axis=0, keepdims=True)
    ref[at, ROW_DIAG:ROW_VK, :] = jnp.broadcast_to(diagonal, (8, DK))
    ref[at, ROW_VK : ROW_VK + DK, :] = vk_first
    ref[at, ROW_VK + DK : ROWS, :] = vk_second


def unpack(ref, at):
    row, col = positions()
    both = ref[at, 0:DK, :]
    turned = both.T
    diagonal = ref[at, ROW_DIAG : ROW_DIAG + 1, :]
    first = jnp.where(row > col, both, jnp.where(row == col, diagonal, turned))
    second = jnp.where(row <= col, both, turned)
    return [first, second], [ref[at, ROW_VK : ROW_VK + DK, :], ref[at, ROW_VK + DK : ROWS, :]]


def head_cols(head):
    return slice(head * DK, (head + 1) * DK)


def sums_kernel(core_ref, k_own, v_own, kv_got, out_ref):
    kk, vk = [], []
    for head in range(2):
        cols = head_cols(head)
        k_all = jnp.concatenate([k_own[:, cols], kv_got[0, :, cols]], axis=0)
        v_all = jnp.concatenate([v_own[:, cols], kv_got[1, :, cols]], axis=0)
        k_split = split(k_all)
        kk.append(mm(split(k_all.T), k_split))
        vk.append(mm(split(v_all.T), k_split))
    pack_into(out_ref, 0, *kk, *vk)


def main_kernel(
    core_ref, q_own, k_own, v_own, g_own, kv_got, qg_got, damp_ref, prior_ref,
    y_own, dq_own, ydq_send, dk_ref, dv_ref, grad_ref, later_ref,
):
    first_core = core_ref[0] == 0
    row, col = positions()
    causal = row <= col

    def mask(x):
        return jnp.where(causal, x, 0.0)

    def blocks(own, got):
        found = []
        for head in range(2):
            cols = head_cols(head)
            mine, other = own[:, cols], got(cols)
            found += [jnp.where(first_core, mine, other), jnp.where(first_core, other, mine)]
        return found

    k = blocks(k_own, lambda cols: kv_got[0, :, cols])
    v = blocks(v_own, lambda cols: kv_got[1, :, cols])
    q_t = each(jnp.transpose, blocks(q_own, lambda cols: qg_got[0, :, cols]))
    g_t = each(jnp.transpose, blocks(g_own, lambda cols: qg_got[1, :, cols]))
    k_s, v_s = each(split, k), each(split, v)
    kt_s = each(lambda x: split(x.T), k)
    vt_s = each(lambda x: split(x.T), v)
    kk_prior, vk_prior = unpack(prior_ref, 0)
    damp, kk, vk = [], [], []
    for head in range(2):
        across = jnp.broadcast_to(damp_ref[0:1, head_cols(head)], (DK, DK)).T
        damp += [across, across]
        early = 2 * head
        kk += [kk_prior[head], kk_prior[head] + mm(kt_s[early], k_s[early])]
        vk += [vk_prior[head], vk_prior[head] + mm(vt_s[early], k_s[early])]
    g_s = each(split, g_t)
    system = each(lambda s, kt: beside(split(s), kt), kk, kt_s)
    to_solved = each(lambda s, kt: beside(split(s.T), kt), vk, kt_s)
    to_out = each(lambda s, vt: beside(split(s), vt), vk, vt_s)

    def total(a, b):
        return jnp.sum(a * b, axis=0, keepdims=True)

    def apply(x):
        x_s = each(split, x)
        scores = each(lambda ks, xs: mask(mm(ks, xs)), k_s, x_s)
        scores_s = each(split, scores)
        image = each(lambda s, xs, ss, d, x1: mm(s, above(xs, ss)) + d * x1, system, x_s, scores_s, damp, x)
        return image, scores, x_s, scores_s

    y_scores_s = each(lambda vs, gs: split(mask(mm(vs, gs))), v_s, g_s)
    x_bar = each(lambda t, gs, ys: mm(t, above(gs, ys)), to_solved, g_s, y_scores_s)

    p0 = q_t
    rho0 = each(total, p0, p0)
    w0, d0, p0_s, d0_s = apply(p0)
    gam0 = each(total, p0, w0)
    al0 = each(lambda a, b: a / b, rho0, gam0)
    r1 = each(lambda p, a, w: p - a * w, p0, al0, w0)
    rho1 = each(total, r1, r1)
    be0 = each(lambda a, b: a / b, rho1, rho0)
    p1 = each(lambda r, b, p: r + b * p, r1, be0, p0)
    w1, d1, p1_s, d1_s = apply(p1)
    gam1 = each(total, p1, w1)
    al1 = each(lambda a, b: a / b, rho1, gam1)
    r2 = each(lambda r, a, w: r - a * w, r1, al1, w1)
    rho2 = each(total, r2, r2)
    be1 = each(lambda a, b: a / b, rho2, rho1)
    p2 = each(lambda r, b, p: r + b * p, r2, be1, p1)
    w2, d2, p2_s, d2_s = apply(p2)
    gam2 = each(total, p2, w2)
    al2 = each(lambda a, b: a / b, rho2, gam2)

    def mix(a0, x0, a1, x1, a2, x2):
        return a0 * x0 + a1 * x1 + a2 * x2

    x_s = each(lambda *a: split(mix(*a)), al0, p0, al1, p1, al2, p2)
    xs_s = each(lambda *a: split(mix(*a)), al0, d0, al1, d1, al2, d2)
    y_t = each(lambda t, xs, ss: mm(t, above(xs, ss)), to_out, x_s, xs_s)
    vk_grad = each(mm_t, g_s, x_s)
    v_grad = each(mm_t, xs_s, g_s)

    ab2 = each(total, x_bar, p2)
    gb2 = each(lambda a, l, g: -a * l / g, ab2, al2, gam2)
    pb2 = each(lambda l, x, g, w: l * x + (2.0 * g) * w, al2, x_bar, gb2, w2)
    bb1 = each(total, pb2, p1)
    rho2b = each(lambda a, g, b, r: a / g + b / r, ab2, gam2, bb1, rho1)
    rb2 = each(lambda p, b, r: p + (2.0 * b) * r, pb2, rho2b, r2)
    ab1 = each(lambda x, p, r, w: jnp.sum(x * p - r * w, axis=0, keepdims=True), x_bar, p1, rb2, w1)
    gb1 = each(lambda a, l, g: -a * l / g, ab1, al1, gam1)
    e2, _, rb2_s, s2_s = apply(rb2)
    pb1 = each(
        lambda l, x, b, p, g, w, e: l * (x - e) + b * p + (2.0 * g) * w, al1, x_bar, be1, pb2, gb1, w1, e2
    )
    bb0 = each(total, pb1, p0)
    rho1b = each(
        lambda b1, be, r1_, a, g, b0, r0: (a / g - b1 * be / r1_) + b0 / r0, bb1, be1, rho1, ab1, gam1, bb0, rho0
    )
    rb1 = each(lambda r, p, b, r1_: r + p + (2.0 * b) * r1_, rb2, pb1, rho1b, r1)
    ab0 = each(lambda x, p, r, w: jnp.sum(x * p - r * w, axis=0, keepdims=True), x_bar, p0, rb1, w0)
    gb0 = each(lambda a, l, g: -a * l / g, ab0, al0, gam0)
    e1, _, rb1_s, s1_s = apply(rb1)
    pb0 = each(
        lambda l, x, b, p, g, w, e: l * (x - e) + b * p + (2.0 * g) * w, al0, x_bar, be0, pb1, gb0, w0, e1
    )
    rho0b = each(lambda a, g, b, be, r: a / g - b * be / r, ab0, gam0, bb0, be0, rho0)
    q_grad = each(lambda p, r, b, q: p + r + (2.0 * b) * q, pb0, rb1, rho0b, p0)

    wb2 = each(lambda g, p: g * p, gb2, p2)
    wb1 = each(lambda g, p, a, r: g * p - a * r, gb1, p1, al1, rb2)
    wb0 = each(lambda g, p, a, r: g * p - a * r, gb0, p0, al0, rb1)
    kk_half = each(
        lambda a, b, c, x, y, z: mm_t(beside(split(a), split(b), split(c)), beside(x, y, z)),
        wb0, wb1, wb2, p0_s, p1_s, p2_s,
    )
    kk_grad = each(lambda x: x + x.T, kk_half)
    k_grad = each(
        lambda d2_, s2, d1_, s1, d0_, ys, b2, p2_, w1_, b1, p1_, a1, w0_, b0, p0_, a0, xs: mm_t(
            beside(d2_, s2, d1_, s1, d0_, ys),
            beside(
                split((2.0 * b2) * p2_), split(-a1 * p1_), split(w1_ + b1 * p1_),
                split(-a0 * p0_), split(w0_ + b0 * p0_), xs,
            ),
        ),
        d2_s, s2_s, d1_s, s1_s, d0_s, y_scores_s, gb2, p2, wb1, gb1, p1, al1, wb0, gb0, p0, al0, x_s,
    )

    for head in range(2):
        cols, early, late = head_cols(head), 2 * head, 2 * head + 1
        dk_ref[0, :, cols] = k_grad[early]
        dk_ref[1, :, cols] = k_grad[late]
        dv_ref[0, :, cols] = v_grad[early]
        dv_ref[1, :, cols] = v_grad[late]
        for values, mine_ref, at in ((y_t, y_own, 0), (q_grad, dq_own, 1)):
            turned = [values[early].T, values[late].T]
            mine_ref[:, cols] = jnp.where(first_core, turned[0], turned[1])
            ydq_send[at, :, cols] = jnp.where(first_core, turned[1], turned[0])
    pack_into(grad_ref, 0, kk_grad[0] + kk_grad[1], kk_grad[2] + kk_grad[3], vk_grad[0] + vk_grad[1], vk_grad[2] + vk_grad[3])
    pack_into(later_ref, 0, kk_grad[1], kk_grad[3], vk_grad[1], vk_grad[3])


def final_kernel(core_ref, k_own, v_own, kv_got, dk_ref, dv_ref, after_ref, later_ref, dk_own, dv_own, send_ref):
    first_core = core_ref[0] == 0
    kk_after, vk_after = unpack(after_ref, 0)
    kk_later, vk_later = unpack(later_ref, 0)
    for head in range(2):
        cols = head_cols(head)
        mine = k_own[:, cols], v_own[:, cols]
        other = kv_got[0, :, cols], kv_got[1, :, cols]
        grads = []
        for at in range(2):
            k, v = (jnp.where(first_core == (at == 0), a, b) for a, b in zip(mine, other))
            kk, vk = kk_after[head], vk_after[head]
            if at == 0:
                kk, vk = kk + kk_later[head], vk + vk_later[head]
            k_s, v_s, kk_s, vk_s = split(k), split(v), split(kk), split(vk)
            dk = dk_ref[at, :, cols] + mm(beside(k_s, v_s), above(kk_s, vk_s))
            dv = dv_ref[at, :, cols] + mm_t(k_s, vk_s)
            grads.append((dk, dv))
        for which, ref in enumerate((dk_own, dv_own)):
            early, late = grads[0][which], grads[1][which]
            ref[:, cols] = jnp.where(first_core, early, late)
            send_ref[which, :, cols] = jnp.where(first_core, late, early)


def call(kernel, pairs, args, in_specs, outs, out_specs, flops):
    traffic = sum(4 * DK * 2 * DK * pairs for _ in args)
    return pl.pallas_call(
        kernel,
        grid_spec=pltpu.PrefetchScalarGridSpec(
            num_scalar_prefetch=1, grid=(pairs,), in_specs=in_specs, out_specs=out_specs
        ),
        out_shape=[jax.ShapeDtypeStruct(shape, f32) for shape in outs],
        compiler_params=pltpu.CompilerParams(vmem_limit_bytes=VMEM_BYTES),
        cost_estimate=pl.CostEstimate(flops=flops * pairs, bytes_accessed=traffic, transcendentals=0),
    )(*args)


def body(queries, key_vectors, value_vectors, damping, grad_output, sub_size):
    assert sub_size == 2 and queries.shape[0] == DK
    core = lax.axis_index("sub")
    chips = lax.axis_size("ctx")
    width = queries.shape[1] // 2
    pairs = width // (2 * DK)
    swap = [(0, 1), (1, 0)]
    core_at = core.reshape(1).astype(jnp.int32)

    def swapped(*arrays):
        theirs = [lax.dynamic_slice(x, (0, (1 - core) * width), (DK, width)) for x in arrays]
        return lax.ppermute(jnp.stack(theirs), "sub", swap)

    kv_got = swapped(key_vectors, value_vectors)
    qg_got = swapped(queries, grad_output)
    damp_row = damping.reshape(1, -1)

    def own_spec(first):
        return pl.BlockSpec((DK, 2 * DK), lambda i, c: (0, c[0] * pairs + first + i))

    def got_spec(first):
        return pl.BlockSpec((2, DK, 2 * DK), lambda i, c: (0, 0, first + i))

    state_spec = pl.BlockSpec((1, ROWS, DK), lambda i, c: (i, 0, 0))
    part_spec = pl.BlockSpec((2, DK, 2 * DK), lambda i, c: (0, 0, i))
    mine_spec = pl.BlockSpec((DK, 2 * DK), lambda i, c: (0, i))

    chunk = 1
    starts = list(range(0, pairs, chunk))
    unit = 2 * DK**3

    results = []
    for first in starts:
        n = min(chunk, pairs - first)
        own, got = own_spec(first), got_spec(first)
        (sums,) = call(
            sums_kernel, n, (core_at, key_vectors, value_vectors, kv_got), [own, own, got],
            [(n, ROWS, DK)], [state_spec], 24 * unit,
        )
        prior = jnp.zeros_like(sums)
        for hop in range(chips - 1):
            prior = prior + lax.ppermute(prior + sums, "ctx", [(hop, hop + 1)])
        damp_spec = pl.BlockSpec((1, 2 * DK), lambda i, c, first=first: (0, c[0] * pairs + first + i))
        wide = n * 2 * DK
        y_own, dq_own, ydq_send, dk, dv, grad, later = call(
            main_kernel, n,
            (core_at, queries, key_vectors, value_vectors, grad_output, kv_got, qg_got, damp_row, prior),
            [own, own, own, own, got, got, damp_spec, state_spec],
            [(DK, wide), (DK, wide), (2, DK, wide), (2, DK, wide), (2, DK, wide), (n, ROWS, DK), (n, ROWS, DK)],
            [mine_spec, mine_spec, part_spec, part_spec, part_spec, state_spec, state_spec],
            4 * 3 * 36 * unit,
        )
        after = jnp.zeros_like(grad)
        for hop in range(chips - 1, 0, -1):
            after = after + lax.ppermute(after + grad, "ctx", [(hop, hop - 1)])
        dk_own, dv_own, send = call(
            final_kernel, n,
            (core_at, key_vectors, value_vectors, kv_got, dk, dv, after, later),
            [own, own, got, part_spec, part_spec, state_spec, state_spec],
            [(DK, wide), (DK, wide), (2, DK, wide)],
            [mine_spec, mine_spec, part_spec],
            4 * 3 * 3 * unit,
        )
        ydq_got = lax.ppermute(ydq_send, "sub", swap)
        dkv_got = lax.ppermute(send, "sub", swap)
        results.append(((y_own, ydq_got[0]), (dq_own, ydq_got[1]), (dk_own, dkv_got[0]), (dv_own, dkv_got[1])))

    def joined(which):
        mine = jnp.concatenate([r[which][0] for r in results], axis=1)
        theirs = jnp.concatenate([r[which][1] for r in results], axis=1)
        left = jnp.where(core == 0, mine, theirs)
        right = jnp.where(core == 0, theirs, mine)
        return jnp.concatenate([left, right], axis=1)

    return tuple(joined(which) for which in range(4))


def solution(mesh):
    split_both = P(("groups", "ctx", "sub"), "head")
    return jax.shard_map(
        functools.partial(body, sub_size=mesh.shape["sub"]),
        mesh=mesh,
        in_specs=(split_both, split_both, split_both, P("head"), split_both),
        out_specs=(split_both,) * 4,
        check_vma=False,
    )
```

```python
import functools

import jax
import jax.numpy as jnp
from jax import lax
from jax.experimental import pallas as pl
from jax.experimental.pallas import tpu as pltpu
from jax.sharding import PartitionSpec as P

DK = 128
ROW_DIAG, ROW_VK, ROWS = DK, DK + 8, 3 * DK + 8
VMEM_BYTES = 12 * 1024 * 1024
COST = 1

f32, bf16 = jnp.float32, jnp.bfloat16


def split(x):
    high = x.astype(bf16)
    return high, (x - high.astype(f32)).astype(bf16)


def each(fn, *lists):
    return [fn(*items) for items in zip(*lists)]


def beside(*parts):
    return tuple(jnp.concatenate(half, axis=1) for half in zip(*parts))


def above(*parts):
    return tuple(jnp.concatenate(half, axis=0) for half in zip(*parts))


def dot(a, b, rhs_dim):
    return lax.dot_general(a, b, (((1,), (rhs_dim,)), ((), ())), preferred_element_type=f32)


def mm(a, b):
    return dot(a[0], b[0], 0) + (dot(a[0], b[1], 0) + dot(a[1], b[0], 0))


def mm_t(a, b):
    return dot(a[0], b[0], 1) + (dot(a[0], b[1], 1) + dot(a[1], b[0], 1))


def positions():
    row = lax.broadcasted_iota(jnp.int32, (DK, DK), 0)
    return row, lax.broadcasted_iota(jnp.int32, (DK, DK), 1)


def pack_into(ref, at, first, second, vk_first, vk_second):
    row, col = positions()
    ref[at, 0:DK, :] = jnp.where(row > col, first, second)
    diagonal = jnp.sum(jnp.where(row == col, first, 0.0), axis=0, keepdims=True)
    ref[at, ROW_DIAG:ROW_VK, :] = jnp.broadcast_to(diagonal, (8, DK))
    ref[at, ROW_VK : ROW_VK + DK, :] = vk_first
    ref[at, ROW_VK + DK : ROWS, :] = vk_second


def unpack(ref, at):
    row, col = positions()
    both = ref[at, 0:DK, :]
    turned = both.T
    diagonal = ref[at, ROW_DIAG : ROW_DIAG + 1, :]
    first = jnp.where(row > col, both, jnp.where(row == col, diagonal, turned))
    second = jnp.where(row <= col, both, turned)
    return [first, second], [ref[at, ROW_VK : ROW_VK + DK, :], ref[at, ROW_VK + DK : ROWS, :]]


def head_cols(head):
    return slice(head * DK, (head + 1) * DK)


def half_cols(half, width, pair, head):
    start = pl.multiple_of(half * width, DK) + (2 * pair + head) * DK
    return pl.ds(pl.multiple_of(start, DK), DK)


def sums_kernel(first, last, core_ref, chip_ref, k_ref, v_ref, k_got, v_got, *rest):
    width = k_got.shape[1]
    if first == 0:
        sums_ref, prior_ref, after_ref = rest
        prior_ref[...] = jnp.zeros_like(prior_ref)
        after_ref[...] = jnp.zeros_like(after_ref)
    else:
        sums_ref = rest[-1]
    for pair in range(first, last):
        kk, vk = [], []
        for head in range(2):
            cols, got = half_cols(core_ref[0], width, pair, head), half_cols(0, width, pair, head)
            k_all = jnp.concatenate([k_ref[:, cols], k_got[:, got]], axis=0)
            v_all = jnp.concatenate([v_ref[:, cols], v_got[:, got]], axis=0)
            k_split = split(k_all)
            kk.append(mm(split(k_all.T), k_split))
            vk.append(mm(split(v_all.T), k_split))
        pack_into(sums_ref, pair, *kk, *vk)


def main_kernel(
    pair, core_ref, chip_ref, q_ref, k_ref, v_ref, g_ref, q_got, k_got, v_got, g_got, damp_ref, prior_ref, *rest,
):
    ydq_own, ydq_send, dkv_own, dkv_send, grad_ref, later_ref = rest[-6:]
    width = k_got.shape[1]
    own_at = [half_cols(core_ref[0], width, pair, head) for head in range(2)]
    got_at = [half_cols(0, width, pair, head) for head in range(2)]
    first_core = core_ref[0] == 0
    row, col = positions()
    causal = row <= col

    def mask(x):
        return jnp.where(causal, x, 0.0)

    def blocks(own, got):
        found = []
        for head in range(2):
            mine, other = own[:, own_at[head]], got[:, got_at[head]]
            found += [jnp.where(first_core, mine, other), jnp.where(first_core, other, mine)]
        return found

    k, v = blocks(k_ref, k_got), blocks(v_ref, v_got)
    q_t, g_t = each(jnp.transpose, blocks(q_ref, q_got)), each(jnp.transpose, blocks(g_ref, g_got))
    k_s, v_s = each(split, k), each(split, v)
    kt_s = each(lambda x: split(x.T), k)
    vt_s = each(lambda x: split(x.T), v)
    kk_prior, vk_prior = unpack(prior_ref, pair)
    damp, kk, vk = [], [], []
    for head in range(2):
        across = jnp.broadcast_to(damp_ref[0:1, own_at[head]], (DK, DK)).T
        damp += [across, across]
        early = 2 * head
        kk += [kk_prior[head], kk_prior[head] + mm(kt_s[early], k_s[early])]
        vk += [vk_prior[head], vk_prior[head] + mm(vt_s[early], k_s[early])]
    g_s = each(split, g_t)
    system = each(lambda s, kt: beside(split(s), kt), kk, kt_s)
    to_solved = each(lambda s, kt: beside(split(s.T), kt), vk, kt_s)
    to_out = each(lambda s, vt: beside(split(s), vt), vk, vt_s)

    def total(a, b):
        return jnp.sum(a * b, axis=0, keepdims=True)

    def apply(x):
        x_s = each(split, x)
        scores = each(lambda ks, xs: mask(mm(ks, xs)), k_s, x_s)
        scores_s = each(split, scores)
        image = each(lambda s, xs, ss, d, x1: mm(s, above(xs, ss)) + d * x1, system, x_s, scores_s, damp, x)
        return image, scores, x_s, scores_s

    y_scores_s = each(lambda vs, gs: split(mask(mm(vs, gs))), v_s, g_s)
    x_bar = each(lambda t, gs, ys: mm(t, above(gs, ys)), to_solved, g_s, y_scores_s)

    p0 = q_t
    rho0 = each(total, p0, p0)
    w0, d0, p0_s, d0_s = apply(p0)
    gam0 = each(total, p0, w0)
    al0 = each(lambda a, b: a / b, rho0, gam0)
    r1 = each(lambda p, a, w: p - a * w, p0, al0, w0)
    rho1 = each(total, r1, r1)
    be0 = each(lambda a, b: a / b, rho1, rho0)
    p1 = each(lambda r, b, p: r + b * p, r1, be0, p0)
    w1, d1, p1_s, d1_s = apply(p1)
    gam1 = each(total, p1, w1)
    al1 = each(lambda a, b: a / b, rho1, gam1)
    r2 = each(lambda r, a, w: r - a * w, r1, al1, w1)
    rho2 = each(total, r2, r2)
    be1 = each(lambda a, b: a / b, rho2, rho1)
    p2 = each(lambda r, b, p: r + b * p, r2, be1, p1)
    w2, d2, p2_s, d2_s = apply(p2)
    gam2 = each(total, p2, w2)
    al2 = each(lambda a, b: a / b, rho2, gam2)

    def mix(a0, x0, a1, x1, a2, x2):
        return a0 * x0 + a1 * x1 + a2 * x2

    x_s = each(lambda *a: split(mix(*a)), al0, p0, al1, p1, al2, p2)
    xs_s = each(lambda *a: split(mix(*a)), al0, d0, al1, d1, al2, d2)
    y_t = each(lambda t, xs, ss: mm(t, above(xs, ss)), to_out, x_s, xs_s)
    vk_grad = each(mm_t, g_s, x_s)
    v_grad = each(mm_t, xs_s, g_s)

    ab2 = each(total, x_bar, p2)
    gb2 = each(lambda a, l, g: -a * l / g, ab2, al2, gam2)
    pb2 = each(lambda l, x, g, w: l * x + (2.0 * g) * w, al2, x_bar, gb2, w2)
    bb1 = each(total, pb2, p1)
    rho2b = each(lambda a, g, b, r: a / g + b / r, ab2, gam2, bb1, rho1)
    rb2 = each(lambda p, b, r: p + (2.0 * b) * r, pb2, rho2b, r2)
    ab1 = each(lambda x, p, r, w: jnp.sum(x * p - r * w, axis=0, keepdims=True), x_bar, p1, rb2, w1)
    gb1 = each(lambda a, l, g: -a * l / g, ab1, al1, gam1)
    e2, _, rb2_s, s2_s = apply(rb2)
    pb1 = each(
        lambda l, x, b, p, g, w, e: l * (x - e) + b * p + (2.0 * g) * w, al1, x_bar, be1, pb2, gb1, w1, e2
    )
    bb0 = each(total, pb1, p0)
    rho1b = each(
        lambda b1, be, r1_, a, g, b0, r0: (a / g - b1 * be / r1_) + b0 / r0, bb1, be1, rho1, ab1, gam1, bb0, rho0
    )
    rb1 = each(lambda r, p, b, r1_: r + p + (2.0 * b) * r1_, rb2, pb1, rho1b, r1)
    ab0 = each(lambda x, p, r, w: jnp.sum(x * p - r * w, axis=0, keepdims=True), x_bar, p0, rb1, w0)
    gb0 = each(lambda a, l, g: -a * l / g, ab0, al0, gam0)
    e1, _, rb1_s, s1_s = apply(rb1)
    pb0 = each(
        lambda l, x, b, p, g, w, e: l * (x - e) + b * p + (2.0 * g) * w, al0, x_bar, be0, pb1, gb0, w0, e1
    )
    rho0b = each(lambda a, g, b, be, r: a / g - b * be / r, ab0, gam0, bb0, be0, rho0)
    q_grad = each(lambda p, r, b, q: p + r + (2.0 * b) * q, pb0, rb1, rho0b, p0)

    wb2 = each(lambda g, p: g * p, gb2, p2)
    wb1 = each(lambda g, p, a, r: g * p - a * r, gb1, p1, al1, rb2)
    wb0 = each(lambda g, p, a, r: g * p - a * r, gb0, p0, al0, rb1)
    kk_half = each(
        lambda a, b, c, x, y, z: mm_t(beside(split(a), split(b), split(c)), beside(x, y, z)),
        wb0, wb1, wb2, p0_s, p1_s, p2_s,
    )
    kk_grad = each(lambda x: x + x.T, kk_half)
    k_grad = each(
        lambda d2_, s2, d1_, s1, d0_, ys, b2, p2_, w1_, b1, p1_, a1, w0_, b0, p0_, a0, xs: mm_t(
            beside(d2_, s2, d1_, s1, d0_, ys),
            beside(
                split((2.0 * b2) * p2_), split(-a1 * p1_), split(w1_ + b1 * p1_),
                split(-a0 * p0_), split(w0_ + b0 * p0_), xs,
            ),
        ),
        d2_s, s2_s, d1_s, s1_s, d0_s, y_scores_s, gb2, p2, wb1, gb1, p1, al1, wb0, gb0, p0, al0, x_s,
    )

    y_grads = each(jnp.transpose, y_t), each(jnp.transpose, q_grad)
    for values, own, send in ((y_grads, ydq_own, ydq_send), ((k_grad, v_grad), dkv_own, dkv_send)):
        for at in range(2):
            for head in range(2):
                early, late = values[at][2 * head], values[at][2 * head + 1]
                own[at, :, got_at[head]] = jnp.where(first_core, early, late)
                send[at, :, got_at[head]] = jnp.where(first_core, late, early)
    kk_both, vk_both = ([x[0] + x[1], x[2] + x[3]] for x in (kk_grad, vk_grad))
    pack_into(grad_ref, pair, *kk_both, *vk_both)
    pack_into(later_ref, pair, kk_grad[1], kk_grad[3], vk_grad[1], vk_grad[3])


def slot_kernel(slot, chips, arrived, sent, turned, pairs, core_ref, chip_ref, *refs):
    refs = list(refs)
    count = {None: 0, "up": 1, "down": 1, "both": 2}
    came = [refs.pop(0)[0] for _ in range(count[arrived])]
    sums, grads, laters, _, _, prior_ref, after_ref = (refs.pop(0) for _ in range(7))
    chip = chip_ref[0]
    even = chip % 2 == 0
    up, down = slot - chip, slot - 2 * chips + 1 + chip
    up_at, down_at = jnp.clip(up, 0, pairs - 1), jnp.clip(down, 0, pairs - 1)
    if arrived in ("up", "both"):

        @pl.when((chip > 0) & (up >= 0) & (up < pairs))
        def _():
            prior_ref[up_at] = came[0] if arrived == "up" else jnp.where(even, came[1], came[0])

    if arrived in ("down", "both"):

        @pl.when((chip < chips - 1) & (down >= 0) & (down < pairs))
        def _():
            after_ref[down_at] = came[0] if arrived == "down" else jnp.where(even, came[0], came[1])

    going = [refs.pop(0) for _ in range(count[sent])]
    if sent in ("up", "both"):
        sent_up = prior_ref[up_at] + sums[up_at]
    if sent in ("down", "both"):
        sent_down = after_ref[down_at] + grads[down_at]
    if sent == "up":
        going[0][0] = sent_up
    if sent == "down":
        going[0][0] = sent_down
    if sent == "both":
        going[0][0] = jnp.where(even, sent_up, sent_down)
        going[1][0] = jnp.where(even, sent_down, sent_up)
    if turned is not None:
        own, other = refs.pop(0), refs.pop(0)
        second = after_ref[turned]
        first = second + laters[turned]
        first_core = core_ref[0] == 0
        own[0] = jnp.where(first_core, first, second)
        other[0] = jnp.where(first_core, second, first)


def final_kernel(pair, core_ref, chip_ref, k_ref, v_ref, dkv_own, dkv_got, after_own, after_got, *rest):
    dk_out, dv_out, dk_at, dv_at, sems = rest[-5:]
    width = dkv_got.shape[2]
    copies = []
    for at, (dkv_ref, after_ref) in enumerate(((dkv_own, after_own), (dkv_got, after_got))):
        half = core_ref[0] if at == 0 else 1 - core_ref[0]
        kk_after, vk_after = unpack(after_ref, 0)
        for head in range(2):
            cols, part, to = half_cols(half, width, pair, head), half_cols(0, width, pair, head), head_cols(head)
            k_s, v_s = split(k_ref[:, cols]), split(v_ref[:, cols])
            kk_s, vk_s = split(kk_after[head]), split(vk_after[head])
            dk_at[at, :, to] = dkv_ref[0, :, part] + mm(beside(k_s, v_s), above(kk_s, vk_s))
            dv_at[at, :, to] = dkv_ref[1, :, part] + mm_t(k_s, vk_s)
        cols = pl.ds(pl.multiple_of(pl.multiple_of(half * width, DK) + 2 * pair * DK, DK), 2 * DK)
        for which, (src, dst) in enumerate(((dk_at, dk_out), (dv_at, dv_out))):
            copies.append(pltpu.make_async_copy(src.at[at], dst.at[:, cols], sems.at[at, which]))
            copies[-1].start()
    for copy in copies:
        copy.wait()


def place_kernel(core_ref, chip_ref, own_ref, got_ref, y_ref, dq_ref, sems):
    width = got_ref.shape[2]
    copies = []
    for which, (half, src) in enumerate(((core_ref[0], own_ref), (1 - core_ref[0], got_ref))):
        cols = pl.ds(pl.multiple_of(half * width, DK), width)
        for at, ref in enumerate((y_ref, dq_ref)):
            copies.append(pltpu.make_async_copy(src.at[at], ref.at[:, cols], sems.at[which, at]))
            copies[-1].start()
    for copy in copies:
        copy.wait()


ANYWHERE = pl.BlockSpec(memory_space=pl.ANY)
LOCAL = pl.BlockSpec(memory_space=pltpu.VMEM)


def call(kernel, grid, args, in_specs, outs, out_specs, flops, aliases=None, scratch=()):
    return pl.pallas_call(
        kernel,
        grid_spec=pltpu.PrefetchScalarGridSpec(
            num_scalar_prefetch=2, grid=(grid,), in_specs=in_specs, out_specs=out_specs, scratch_shapes=scratch
        ),
        out_shape=[jax.ShapeDtypeStruct(shape, f32) for shape in outs],
        input_output_aliases=aliases or {},
        compiler_params=pltpu.CompilerParams(vmem_limit_bytes=VMEM_BYTES),
        cost_estimate=pl.CostEstimate(flops=COST, bytes_accessed=COST, transcendentals=0),
    )(*args)


def body(queries, key_vectors, value_vectors, damping, grad_output, sub_size):
    assert sub_size == 2 and queries.shape[0] == DK
    core = lax.axis_index("sub")
    chips = lax.axis_size("ctx")
    whole = queries.shape[1]
    width = whole // 2
    pairs = width // (2 * DK)
    swap = [(0, 1), (1, 0)]
    at = tuple(lax.axis_index(name).astype(jnp.int32).reshape(1) for name in ("sub", "ctx"))
    unit = 2 * DK**3

    def swapped(*arrays):
        theirs = [lax.dynamic_slice(x, (0, (1 - core) * width), (DK, width)) for x in arrays]
        return [lax.ppermute(x, "sub", swap) for x in theirs]

    k_got, v_got = swapped(key_vectors, value_vectors)
    q_got, g_got = swapped(queries, grad_output)

    state_shape, states_shape = (1, ROWS, DK), (pairs, ROWS, DK)
    damp_row = damping.reshape(1, -1)
    near_pairs = [(a, a ^ 1 if a ^ 1 < chips else a) for a in range(chips)]
    far_pairs = [(a, b if 0 <= b < chips else a) for a in range(chips) for b in [a - 1 if a % 2 == 0 else a + 1]]

    done = []

    def after(x):
        return lax.optimization_barrier((x, *done))[0] if done else x

    def mark(x):
        done[:] = [x]
        return x

    exchanges = {
        "up": [[(a, (a + 1) % chips) for a in range(chips)]],
        "down": [[((a + 1) % chips, a) for a in range(chips)]],
        "both": [near_pairs, far_pairs],
    }

    kv = key_vectors, value_vectors, k_got, v_got
    sums, prior, later_sums = call(
        functools.partial(sums_kernel, 0, 1), 1, (*at, *kv), [LOCAL] * 4, [states_shape] * 3, [LOCAL] * 3, 1
    )
    grad, later = later_sums, later_sums
    bulk, grads, arrived, waiting = (), (), None, []
    came = ()

    def run_final(pair, after_own, after_got):
        nonlocal grads
        grads = call(
            functools.partial(final_kernel, pair), 1,
            (*at, key_vectors, value_vectors, bulk[2], dkv_got, after(after_own), after_got, *grads),
            [LOCAL] * 6 + [ANYWHERE] * len(grads), [(DK, whole)] * 2, [ANYWHERE] * 2, 1,
            aliases={8: 0, 9: 1} if grads else None,
            scratch=[pltpu.VMEM((2, DK, 2 * DK), f32)] * 2 + [pltpu.SemaphoreType.DMA((2, 2))],
        )
        mark(grads[0])

    last_up, last_down = pairs + chips - 3, pairs + 2 * chips - 3
    for slot in range(last_down + 2):
        up, down = slot <= last_up, chips <= slot <= last_down
        sent = "both" if up and down else "up" if up else "down" if down else None
        turned = slot - 2 * chips + 1
        turned = turned if 0 <= turned < pairs else None
        ways = len(exchanges.get(sent, ()))
        extra = ways + 2 * (turned is not None)
        n = len(came)
        outs = call(
            functools.partial(slot_kernel, slot, chips, arrived, sent, turned, pairs), 1,
            (*at, *came, sums, grad, later, prior, after(later_sums)),
            [LOCAL] * (n + 5), [states_shape] * 2 + [state_shape] * extra, [LOCAL] * (2 + extra), 1,
            aliases={n + 5: 0, n + 6: 1},
        )
        prior, later_sums, *outs = outs
        mark(prior)
        came = [lax.ppermute(outs.pop(0), "ctx", pairing) for pairing in exchanges.get(sent, ())]
        arrived = sent
        if turned is not None:
            waiting.append((turned, outs[0], lax.ppermute(outs[1], "sub", swap)))
        if slot == last_down:
            y, dq = call(
                place_kernel, 1, (*at, bulk[0], after(ydq_got)), [LOCAL] * 2, [(DK, whole)] * 2, [ANYWHERE] * 2, 1,
                scratch=[pltpu.SemaphoreType.DMA((2, 2))],
            )
            mark(y)
        while waiting and (slot > last_down or (slot == last_down and len(waiting) > 1)):
            run_final(*waiting.pop(0))
        if slot == 0 and pairs > 1:
            (sums,) = call(
                functools.partial(sums_kernel, 1, pairs), 1, (*at, *kv, after(sums)), [LOCAL] * 5, [states_shape], [LOCAL], 1,
                aliases={6: 0},
            )
            mark(sums)
        pair = slot - chips + 1
        if 0 <= pair < pairs:
            carried = (*bulk, grad, later) if bulk else ()
            outs = call(
                functools.partial(main_kernel, pair), 1,
                (*at, queries, key_vectors, value_vectors, grad_output, q_got, k_got, v_got, g_got, damp_row, after(prior), *carried),
                [LOCAL] * (10 + len(carried)), [(2, DK, width)] * 4 + [states_shape] * 2, [LOCAL] * 6, 1,
                aliases={12 + k: k for k in range(6)} if carried else None,
            )
            *bulk, grad, later = outs
            mark(grad)
        if slot == last_down - 1:
            dkv_got = lax.ppermute(after(bulk[3]), "sub", swap)
            ydq_got = lax.ppermute(after(bulk[1]), "sub", swap)
    return (y, dq, *grads)


def solution(mesh):
    split_both = P(("groups", "ctx", "sub"), "head")
    return jax.shard_map(
        functools.partial(body, sub_size=mesh.shape["sub"]),
        mesh=mesh,
        in_specs=(split_both, split_both, split_both, P("head"), split_both),
        out_specs=(split_both,) * 4,
        check_vma=False,
    )
```

```python
import functools

import jax
import jax.numpy as jnp
from jax import lax
from jax.experimental import pallas as pl
from jax.experimental.pallas import tpu as pltpu
from jax.sharding import PartitionSpec as P

DK = 128
ROW_DIAG, ROW_VK, ROWS = DK, DK + 8, 3 * DK + 8
VMEM_BYTES = 12 * 1024 * 1024
COST = 1

f32, bf16 = jnp.float32, jnp.bfloat16


def split(x):
    high = x.astype(bf16)
    return high, (x - high.astype(f32)).astype(bf16)


def each(fn, *lists):
    return [fn(*items) for items in zip(*lists)]


def beside(*parts):
    return tuple(jnp.concatenate(half, axis=1) for half in zip(*parts))


def above(*parts):
    return tuple(jnp.concatenate(half, axis=0) for half in zip(*parts))


def dot(a, b, rhs_dim):
    return lax.dot_general(a, b, (((1,), (rhs_dim,)), ((), ())), preferred_element_type=f32)


def mm(a, b):
    high = dot(a[0], jnp.concatenate(b, axis=1), 0)
    return high[:, :DK] + (high[:, DK:] + dot(a[1], b[0], 0))


def mm_t(a, b):
    high = dot(a[0], jnp.concatenate(b, axis=0), 1)
    return high[:, :DK] + (high[:, DK:] + dot(a[1], b[0], 1))


def positions():
    row = lax.broadcasted_iota(jnp.int32, (DK, DK), 0)
    return row, lax.broadcasted_iota(jnp.int32, (DK, DK), 1)


def pack_into(ref, at, first, second, vk_first, vk_second):
    row, col = positions()
    ref[at, 0:DK, :] = jnp.where(row > col, first, second)
    diagonal = jnp.sum(jnp.where(row == col, first, 0.0), axis=0, keepdims=True)
    ref[at, ROW_DIAG:ROW_VK, :] = jnp.broadcast_to(diagonal, (8, DK))
    ref[at, ROW_VK : ROW_VK + DK, :] = vk_first
    ref[at, ROW_VK + DK : ROWS, :] = vk_second


def unpack(ref, at):
    row, col = positions()
    both = ref[at, 0:DK, :]
    turned = both.T
    diagonal = ref[at, ROW_DIAG : ROW_DIAG + 1, :]
    first = jnp.where(row > col, both, jnp.where(row == col, diagonal, turned))
    second = jnp.where(row <= col, both, turned)
    return [first, second], [ref[at, ROW_VK : ROW_VK + DK, :], ref[at, ROW_VK + DK : ROWS, :]]


def head_cols(head):
    return slice(head * DK, (head + 1) * DK)


def half_cols(half, width, pair, head):
    start = pl.multiple_of(half * width, DK) + (2 * pair + head) * DK
    return pl.ds(pl.multiple_of(start, DK), DK)


def sums_kernel(first, last, core_ref, chip_ref, k_ref, v_ref, k_got, v_got, *rest):
    width = k_got.shape[1]
    if first == 0:
        sums_ref, prior_ref, after_ref = rest
        prior_ref[...] = jnp.zeros_like(prior_ref)
        after_ref[...] = jnp.zeros_like(after_ref)
    else:
        sums_ref = rest[-1]
    for pair in range(first, last):
        kk, vk = [], []
        for head in range(2):
            cols, got = half_cols(core_ref[0], width, pair, head), half_cols(0, width, pair, head)
            k_all = jnp.concatenate([k_ref[:, cols], k_got[:, got]], axis=0)
            v_all = jnp.concatenate([v_ref[:, cols], v_got[:, got]], axis=0)
            k_split = split(k_all)
            kk.append(mm(split(k_all.T), k_split))
            vk.append(mm(split(v_all.T), k_split))
        pack_into(sums_ref, pair, *kk, *vk)


def main_kernel(
    pair, core_ref, chip_ref, q_ref, k_ref, v_ref, g_ref, q_got, k_got, v_got, g_got, damp_ref, prior_ref, *rest,
):
    ydq_own, ydq_send, dkv_own, dkv_send, grad_ref, later_ref = rest[-6:]
    width = k_got.shape[1]
    own_at = [half_cols(core_ref[0], width, pair, head) for head in range(2)]
    got_at = [half_cols(0, width, pair, head) for head in range(2)]
    first_core = core_ref[0] == 0
    row, col = positions()
    causal = row <= col

    def mask(x):
        return jnp.where(causal, x, 0.0)

    def blocks(own, got):
        found = []
        for head in range(2):
            mine, other = own[:, own_at[head]], got[:, got_at[head]]
            found += [jnp.where(first_core, mine, other), jnp.where(first_core, other, mine)]
        return found

    k, v = blocks(k_ref, k_got), blocks(v_ref, v_got)
    q_t, g_t = each(jnp.transpose, blocks(q_ref, q_got)), each(jnp.transpose, blocks(g_ref, g_got))
    k_s, v_s = each(split, k), each(split, v)
    kt_s = each(lambda x: split(x.T), k)
    vt_s = each(lambda x: split(x.T), v)
    kk_prior, vk_prior = unpack(prior_ref, pair)
    damp, kk, vk = [], [], []
    for head in range(2):
        across = jnp.broadcast_to(damp_ref[0:1, own_at[head]], (DK, DK)).T
        damp += [across, across]
        early = 2 * head
        kk += [kk_prior[head], kk_prior[head] + mm(kt_s[early], k_s[early])]
        vk += [vk_prior[head], vk_prior[head] + mm(vt_s[early], k_s[early])]
    g_s = each(split, g_t)
    system = each(lambda s, kt: beside(split(s), kt), kk, kt_s)
    to_solved = each(lambda s, kt: beside(split(s.T), kt), vk, kt_s)
    to_out = each(lambda s, vt: beside(split(s), vt), vk, vt_s)

    def total(a, b):
        return jnp.sum(a * b, axis=0, keepdims=True)

    def apply(x):
        x_s = each(split, x)
        scores = each(lambda ks, xs: mask(mm(ks, xs)), k_s, x_s)
        scores_s = each(split, scores)
        image = each(lambda s, xs, ss, d, x1: mm(s, above(xs, ss)) + d * x1, system, x_s, scores_s, damp, x)
        return image, scores, x_s, scores_s

    y_scores_s = each(lambda vs, gs: split(mask(mm(vs, gs))), v_s, g_s)
    x_bar = each(lambda t, gs, ys: mm(t, above(gs, ys)), to_solved, g_s, y_scores_s)

    p0 = q_t
    rho0 = each(total, p0, p0)
    w0, d0, p0_s, d0_s = apply(p0)
    gam0 = each(total, p0, w0)
    al0 = each(lambda a, b: a / b, rho0, gam0)
    r1 = each(lambda p, a, w: p - a * w, p0, al0, w0)
    rho1 = each(total, r1, r1)
    be0 = each(lambda a, b: a / b, rho1, rho0)
    p1 = each(lambda r, b, p: r + b * p, r1, be0, p0)
    w1, d1, p1_s, d1_s = apply(p1)
    gam1 = each(total, p1, w1)
    al1 = each(lambda a, b: a / b, rho1, gam1)
    r2 = each(lambda r, a, w: r - a * w, r1, al1, w1)
    rho2 = each(total, r2, r2)
    be1 = each(lambda a, b: a / b, rho2, rho1)
    p2 = each(lambda r, b, p: r + b * p, r2, be1, p1)
    w2, d2, p2_s, d2_s = apply(p2)
    gam2 = each(total, p2, w2)
    al2 = each(lambda a, b: a / b, rho2, gam2)

    def mix(a0, x0, a1, x1, a2, x2):
        return a0 * x0 + a1 * x1 + a2 * x2

    x_s = each(lambda *a: split(mix(*a)), al0, p0, al1, p1, al2, p2)
    xs_s = each(lambda *a: split(mix(*a)), al0, d0, al1, d1, al2, d2)
    y_t = each(lambda t, xs, ss: mm(t, above(xs, ss)), to_out, x_s, xs_s)
    vk_grad = each(mm_t, g_s, x_s)
    v_grad = each(mm_t, xs_s, g_s)

    ab2 = each(total, x_bar, p2)
    gb2 = each(lambda a, l, g: -a * l / g, ab2, al2, gam2)
    pb2 = each(lambda l, x, g, w: l * x + (2.0 * g) * w, al2, x_bar, gb2, w2)
    bb1 = each(total, pb2, p1)
    rho2b = each(lambda a, g, b, r: a / g + b / r, ab2, gam2, bb1, rho1)
    rb2 = each(lambda p, b, r: p + (2.0 * b) * r, pb2, rho2b, r2)
    ab1 = each(lambda x, p, r, w: jnp.sum(x * p - r * w, axis=0, keepdims=True), x_bar, p1, rb2, w1)
    gb1 = each(lambda a, l, g: -a * l / g, ab1, al1, gam1)
    e2, _, rb2_s, s2_s = apply(rb2)
    pb1 = each(
        lambda l, x, b, p, g, w, e: l * (x - e) + b * p + (2.0 * g) * w, al1, x_bar, be1, pb2, gb1, w1, e2
    )
    bb0 = each(total, pb1, p0)
    rho1b = each(
        lambda b1, be, r1_, a, g, b0, r0: (a / g - b1 * be / r1_) + b0 / r0, bb1, be1, rho1, ab1, gam1, bb0, rho0
    )
    rb1 = each(lambda r, p, b, r1_: r + p + (2.0 * b) * r1_, rb2, pb1, rho1b, r1)
    ab0 = each(lambda x, p, r, w: jnp.sum(x * p - r * w, axis=0, keepdims=True), x_bar, p0, rb1, w0)
    gb0 = each(lambda a, l, g: -a * l / g, ab0, al0, gam0)
    e1, _, rb1_s, s1_s = apply(rb1)
    pb0 = each(
        lambda l, x, b, p, g, w, e: l * (x - e) + b * p + (2.0 * g) * w, al0, x_bar, be0, pb1, gb0, w0, e1
    )
    rho0b = each(lambda a, g, b, be, r: a / g - b * be / r, ab0, gam0, bb0, be0, rho0)
    q_grad = each(lambda p, r, b, q: p + r + (2.0 * b) * q, pb0, rb1, rho0b, p0)

    wb2 = each(lambda g, p: g * p, gb2, p2)
    wb1 = each(lambda g, p, a, r: g * p - a * r, gb1, p1, al1, rb2)
    wb0 = each(lambda g, p, a, r: g * p - a * r, gb0, p0, al0, rb1)
    kk_half = each(
        lambda a, b, c, x, y, z: mm_t(beside(split(a), split(b), split(c)), beside(x, y, z)),
        wb0, wb1, wb2, p0_s, p1_s, p2_s,
    )
    kk_grad = each(lambda x: x + x.T, kk_half)
    k_grad = each(
        lambda d2_, s2, d1_, s1, d0_, ys, b2, p2_, w1_, b1, p1_, a1, w0_, b0, p0_, a0, xs: mm_t(
            beside(d2_, s2, d1_, s1, d0_, ys),
            beside(
                split((2.0 * b2) * p2_), split(-a1 * p1_), split(w1_ + b1 * p1_),
                split(-a0 * p0_), split(w0_ + b0 * p0_), xs,
            ),
        ),
        d2_s, s2_s, d1_s, s1_s, d0_s, y_scores_s, gb2, p2, wb1, gb1, p1, al1, wb0, gb0, p0, al0, x_s,
    )

    y_grads = each(jnp.transpose, y_t), each(jnp.transpose, q_grad)
    for values, own, send in ((y_grads, ydq_own, ydq_send), ((k_grad, v_grad), dkv_own, dkv_send)):
        for at in range(2):
            for head in range(2):
                early, late = values[at][2 * head], values[at][2 * head + 1]
                own[at, :, got_at[head]] = jnp.where(first_core, early, late)
                send[at, :, got_at[head]] = jnp.where(first_core, late, early)
    kk_both, vk_both = ([x[0] + x[1], x[2] + x[3]] for x in (kk_grad, vk_grad))
    pack_into(grad_ref, pair, *kk_both, *vk_both)
    pack_into(later_ref, pair, kk_grad[1], kk_grad[3], vk_grad[1], vk_grad[3])


def slot_kernel(slot, chips, arrived, sent, turned, pairs, core_ref, chip_ref, *refs):
    refs = list(refs)
    count = {None: 0, "up": 1, "down": 1, "both": 2}
    came = [refs.pop(0)[0] for _ in range(count[arrived])]
    sums, grads, laters, _, _, prior_ref, after_ref = (refs.pop(0) for _ in range(7))
    chip = chip_ref[0]
    even = chip % 2 == 0
    up, down = slot - chip, slot - 2 * chips + 1 + chip
    up_at, down_at = jnp.clip(up, 0, pairs - 1), jnp.clip(down, 0, pairs - 1)
    if arrived in ("up", "both"):

        @pl.when((chip > 0) & (up >= 0) & (up < pairs))
        def _():
            prior_ref[up_at] = came[0] if arrived == "up" else jnp.where(even, came[1], came[0])

    if arrived in ("down", "both"):

        @pl.when((chip < chips - 1) & (down >= 0) & (down < pairs))
        def _():
            after_ref[down_at] = came[0] if arrived == "down" else jnp.where(even, came[0], came[1])

    going = [refs.pop(0) for _ in range(count[sent])]
    if sent in ("up", "both"):
        sent_up = prior_ref[up_at] + sums[up_at]
    if sent in ("down", "both"):
        sent_down = after_ref[down_at] + grads[down_at]
    if sent == "up":
        going[0][0] = sent_up
    if sent == "down":
        going[0][0] = sent_down
    if sent == "both":
        going[0][0] = jnp.where(even, sent_up, sent_down)
        going[1][0] = jnp.where(even, sent_down, sent_up)
    if turned is not None:
        own, other = refs.pop(0), refs.pop(0)
        second = after_ref[turned]
        first = second + laters[turned]
        first_core = core_ref[0] == 0
        own[0] = jnp.where(first_core, first, second)
        other[0] = jnp.where(first_core, second, first)


def final_kernel(pair, core_ref, chip_ref, k_ref, v_ref, dkv_own, dkv_got, after_own, after_got, *rest):
    dk_out, dv_out, dk_at, dv_at, sems = rest[-5:]
    width = dkv_got.shape[2]
    copies = []
    for at, (dkv_ref, after_ref) in enumerate(((dkv_own, after_own), (dkv_got, after_got))):
        half = core_ref[0] if at == 0 else 1 - core_ref[0]
        kk_after, vk_after = unpack(after_ref, 0)
        for head in range(2):
            cols, part, to = half_cols(half, width, pair, head), half_cols(0, width, pair, head), head_cols(head)
            k_s, v_s = split(k_ref[:, cols]), split(v_ref[:, cols])
            kk_s, vk_s = split(kk_after[head]), split(vk_after[head])
            dk_at[at, :, to] = dkv_ref[0, :, part] + mm(beside(k_s, v_s), above(kk_s, vk_s))
            dv_at[at, :, to] = dkv_ref[1, :, part] + mm_t(k_s, vk_s)
        cols = pl.ds(pl.multiple_of(pl.multiple_of(half * width, DK) + 2 * pair * DK, DK), 2 * DK)
        for which, (src, dst) in enumerate(((dk_at, dk_out), (dv_at, dv_out))):
            copies.append(pltpu.make_async_copy(src.at[at], dst.at[:, cols], sems.at[at, which]))
            copies[-1].start()
    for copy in copies:
        copy.wait()


def halves_kernel(core_ref, chip_ref, a_ref, b_ref, a_half, b_half, sems):
    width = a_half.shape[1]
    cols = pl.ds(pl.multiple_of((1 - core_ref[0]) * width, DK), width)
    copies = [
        pltpu.make_async_copy(src.at[:, cols], dst, sems.at[which])
        for which, (src, dst) in enumerate(((a_ref, a_half), (b_ref, b_half)))
    ]
    for copy in copies:
        copy.start()
    for copy in copies:
        copy.wait()


def place_kernel(core_ref, chip_ref, own_ref, got_ref, y_ref, dq_ref, sems):
    width = got_ref.shape[2]
    copies = []
    for which, (half, src) in enumerate(((core_ref[0], own_ref), (1 - core_ref[0], got_ref))):
        cols = pl.ds(pl.multiple_of(half * width, DK), width)
        for at, ref in enumerate((y_ref, dq_ref)):
            copies.append(pltpu.make_async_copy(src.at[at], ref.at[:, cols], sems.at[which, at]))
            copies[-1].start()
    for copy in copies:
        copy.wait()


ANYWHERE = pl.BlockSpec(memory_space=pl.ANY)
LOCAL = pl.BlockSpec(memory_space=pltpu.VMEM)
REMOTE = pl.BlockSpec(memory_space=pltpu.HBM)


def call(kernel, grid, args, in_specs, outs, out_specs, flops, aliases=None, scratch=()):
    return pl.pallas_call(
        kernel,
        grid_spec=pltpu.PrefetchScalarGridSpec(
            num_scalar_prefetch=2, grid=(grid,), in_specs=in_specs, out_specs=out_specs, scratch_shapes=scratch
        ),
        out_shape=[jax.ShapeDtypeStruct(shape, f32) for shape in outs],
        input_output_aliases=aliases or {},
        compiler_params=pltpu.CompilerParams(vmem_limit_bytes=VMEM_BYTES),
        cost_estimate=pl.CostEstimate(flops=COST, bytes_accessed=COST, transcendentals=0),
    )(*args)


def body(queries, key_vectors, value_vectors, damping, grad_output, sub_size):
    assert sub_size == 2 and queries.shape[0] == DK
    core = lax.axis_index("sub")
    chips = lax.axis_size("ctx")
    whole = queries.shape[1]
    width = whole // 2
    pairs = width // (2 * DK)
    swap = [(0, 1), (1, 0)]
    at = tuple(lax.axis_index(name).astype(jnp.int32).reshape(1) for name in ("sub", "ctx"))
    unit = 2 * DK**3

    def swapped(a, b):
        halves = call(
            halves_kernel, 1, (*at, a, b), [REMOTE] * 2, [(DK, width)] * 2, [LOCAL] * 2, 1,
            scratch=[pltpu.SemaphoreType.DMA((2,))],
        )
        return [lax.ppermute(x, "sub", swap) for x in halves]

    k_got, v_got = swapped(key_vectors, value_vectors)
    q_got, g_got = swapped(queries, grad_output)

    state_shape, states_shape = (1, ROWS, DK), (pairs, ROWS, DK)
    damp_row = damping.reshape(1, -1)

    def exchanges(slot, sent):
        ups = [(a, a + 1) for a in range(chips - 1) if 0 <= slot - a < pairs]
        downs = [(b, b - 1) for b in range(1, chips) if 0 <= slot - 2 * chips + 1 + b < pairs]
        if sent == "both":
            near = [(a, a ^ 1 if a ^ 1 < chips else a) for a in range(chips)]
            far = [(a, b if 0 <= b < chips else a) for a in range(chips) for b in [a - 1 if a % 2 == 0 else a + 1]]
            return [near, far]
        links = ups if sent == "up" else downs
        if len(links) < 2 or chips < 3:
            return [links]
        step = 1 if sent == "up" else -1
        return [[(a, (a + step) % chips) for a in range(chips)]]

    done = []

    def after(x):
        return lax.optimization_barrier((x, *done))[0] if done else x

    def mark(x):
        done[:] = [x]
        return x

    kv = key_vectors, value_vectors, k_got, v_got
    sums, prior, later_sums = call(
        functools.partial(sums_kernel, 0, 1), 1, (*at, *kv), [LOCAL] * 4, [states_shape] * 3, [LOCAL] * 3, 1
    )
    grad, later = later_sums, later_sums
    bulk, grads, arrived, waiting = (), (), None, []
    came = ()

    def run_final(pair, after_own, after_got):
        nonlocal grads
        grads = call(
            functools.partial(final_kernel, pair), 1,
            (*at, key_vectors, value_vectors, bulk[2], dkv_got, after(after_own), after_got, *grads),
            [LOCAL] * 6 + [ANYWHERE] * len(grads), [(DK, whole)] * 2, [ANYWHERE] * 2, 1,
            aliases={8: 0, 9: 1} if grads else None,
            scratch=[pltpu.VMEM((2, DK, 2 * DK), f32)] * 2 + [pltpu.SemaphoreType.DMA((2, 2))],
        )
        mark(grads[0])

    last_up, last_down = pairs + chips - 3, pairs + 2 * chips - 3
    for slot in range(last_down + 2):
        up, down = slot <= last_up, chips <= slot <= last_down
        sent = "both" if up and (down or slot >= chips - 2) else "up" if up else "down" if down else None
        turned = slot - 2 * chips + 1
        turned = turned if 0 <= turned < pairs else None
        ways = {None: 0, "both": 2}.get(sent, 1)
        extra = ways + 2 * (turned is not None)
        n = len(came)
        outs = call(
            functools.partial(slot_kernel, slot, chips, arrived, sent, turned, pairs), 1,
            (*at, *came, sums, grad, later, prior, after(later_sums)),
            [LOCAL] * (n + 5), [states_shape] * 2 + [state_shape] * extra, [LOCAL] * (2 + extra), 1,
            aliases={n + 5: 0, n + 6: 1},
        )
        prior, later_sums, *outs = outs
        mark(prior)
        came = [lax.ppermute(outs.pop(0), "ctx", pairing) for pairing in (exchanges(slot, sent) if sent else ())]
        arrived = sent
        if turned is not None:
            waiting.append((turned, outs[0], lax.ppermute(outs[1], "sub", swap)))
        if slot == last_down:
            y, dq = call(
                place_kernel, 1, (*at, bulk[0], after(ydq_got)), [LOCAL] * 2, [(DK, whole)] * 2, [ANYWHERE] * 2, 1,
                scratch=[pltpu.SemaphoreType.DMA((2, 2))],
            )
            mark(y)
        while waiting and (slot > last_down or (slot == last_down and len(waiting) > 1)):
            run_final(*waiting.pop(0))
        if slot == 0 and pairs > 1:
            (sums,) = call(
                functools.partial(sums_kernel, 1, pairs), 1, (*at, *kv, after(sums)), [LOCAL] * 5, [states_shape], [LOCAL], 1,
                aliases={6: 0},
            )
            mark(sums)
        pair = slot - chips + 1
        if 0 <= pair < pairs:
            carried = (*bulk, grad, later) if bulk else ()
            outs = call(
                functools.partial(main_kernel, pair), 1,
                (*at, queries, key_vectors, value_vectors, grad_output, q_got, k_got, v_got, g_got, damp_row, after(prior), *carried),
                [LOCAL] * (10 + len(carried)), [(2, DK, width)] * 4 + [states_shape] * 2, [LOCAL] * 6, 1,
                aliases={12 + k: k for k in range(6)} if carried else None,
            )
            *bulk, grad, later = outs
            mark(grad)
        if slot == last_down - 1:
            dkv_got = lax.ppermute(after(bulk[3]), "sub", swap)
            ydq_got = lax.ppermute(after(bulk[1]), "sub", swap)
    return (y, dq, *grads)


def solution(mesh):
    split_both = P(("groups", "ctx", "sub"), "head")
    return jax.shard_map(
        functools.partial(body, sub_size=mesh.shape["sub"]),
        mesh=mesh,
        in_specs=(split_both, split_both, split_both, P("head"), split_both),
        out_specs=(split_both,) * 4,
        check_vma=False,
    )
```

```python
import functools

import jax
import jax.numpy as jnp
from jax import lax
from jax.experimental import pallas as pl
from jax.experimental.pallas import tpu as pltpu
from jax.sharding import PartitionSpec as P

DK = 128
ROW_DIAG, ROW_VK, ROWS = DK, DK + 8, 3 * DK + 8
VMEM_BYTES = 12 * 1024 * 1024
COST = 1

f32, bf16 = jnp.float32, jnp.bfloat16


def split(x):
    high = x.astype(bf16)
    return high, (x - high.astype(f32)).astype(bf16)


def each(fn, *lists):
    return [fn(*items) for items in zip(*lists)]


def beside(*parts):
    return tuple(jnp.concatenate(half, axis=1) for half in zip(*parts))


def above(*parts):
    return tuple(jnp.concatenate(half, axis=0) for half in zip(*parts))


def dot(a, b, rhs_dim):
    return lax.dot_general(a, b, (((1,), (rhs_dim,)), ((), ())), preferred_element_type=f32)


def mm(a, b):
    if a[0].shape[1] == DK:
        once = jnp.concatenate(b, axis=1)
        sides = dot(jnp.concatenate(a, axis=1), jnp.concatenate([once, once], axis=0), 0)
        return sides[:, :DK] + sides[:, DK:]
    high = dot(a[0], jnp.concatenate(b, axis=1), 0)
    return high[:, :DK] + (high[:, DK:] + dot(a[1], b[0], 0))


def mm_t(a, b):
    if a[0].shape[1] == DK:
        once = jnp.concatenate(b, axis=0)
        sides = dot(jnp.concatenate(a, axis=1), jnp.concatenate([once, once], axis=1), 1)
        return sides[:, :DK] + sides[:, DK:]
    high = dot(a[0], jnp.concatenate(b, axis=0), 1)
    return high[:, :DK] + (high[:, DK:] + dot(a[1], b[0], 1))


def positions():
    row = lax.broadcasted_iota(jnp.int32, (DK, DK), 0)
    return row, lax.broadcasted_iota(jnp.int32, (DK, DK), 1)


def pack_into(ref, at, first, second, vk_first, vk_second):
    row, col = positions()
    ref[at, 0:DK, :] = jnp.where(row > col, first, second)
    diagonal = jnp.sum(jnp.where(row == col, first, 0.0), axis=0, keepdims=True)
    ref[at, ROW_DIAG:ROW_VK, :] = jnp.broadcast_to(diagonal, (8, DK))
    ref[at, ROW_VK : ROW_VK + DK, :] = vk_first
    ref[at, ROW_VK + DK : ROWS, :] = vk_second


def unpack(ref, at):
    row, col = positions()
    both = ref[at, 0:DK, :]
    turned = both.T
    diagonal = ref[at, ROW_DIAG : ROW_DIAG + 1, :]
    first = jnp.where(row > col, both, jnp.where(row == col, diagonal, turned))
    second = jnp.where(row <= col, both, turned)
    return [first, second], [ref[at, ROW_VK : ROW_VK + DK, :], ref[at, ROW_VK + DK : ROWS, :]]


def head_cols(head):
    return slice(head * DK, (head + 1) * DK)


def half_cols(half, width, pair, head):
    start = pl.multiple_of(half * width, DK) + (2 * pair + head) * DK
    return pl.ds(pl.multiple_of(start, DK), DK)


def first_kernel(core_ref, chip_ref, k_own, v_own, k_other, v_other, own_ref, other_ref):
    for k_ref, v_ref, out_ref in ((k_own, v_own, own_ref), (k_other, v_other, other_ref)):
        kk, vk = [], []
        for head in range(2):
            k, v = k_ref[:, head_cols(head)], v_ref[:, head_cols(head)]
            k_split = split(k)
            kk.append(mm(split(k.T), k_split))
            vk.append(mm(split(v.T), k_split))
        pack_into(out_ref, 0, *kk, *vk)


def start_kernel(core_ref, chip_ref, own_ref, got_ref, sums_ref, prior_ref, after_ref):
    prior_ref[...] = jnp.zeros_like(prior_ref)
    after_ref[...] = jnp.zeros_like(after_ref)
    sums_ref[...] = jnp.zeros_like(sums_ref)
    sums_ref[0] = own_ref[0] + got_ref[0]


def sums_kernel(first, last, core_ref, chip_ref, k_ref, v_ref, k_got, v_got, *rest):
    width = k_got.shape[1]
    sums_ref = rest[-1]
    for pair in range(first, last):
        kk, vk = [], []
        for head in range(2):
            cols, got = half_cols(core_ref[0], width, pair, head), half_cols(0, width, pair, head)
            k_all = jnp.concatenate([k_ref[:, cols], k_got[:, got]], axis=0)
            v_all = jnp.concatenate([v_ref[:, cols], v_got[:, got]], axis=0)
            k_split = split(k_all)
            kk.append(mm(split(k_all.T), k_split))
            vk.append(mm(split(v_all.T), k_split))
        pack_into(sums_ref, pair, *kk, *vk)


def main_kernel(
    pair, core_ref, chip_ref, q_ref, k_ref, v_ref, g_ref, q_got, k_got, v_got, g_got, damp_ref, prior_ref, *rest,
):
    ydq_own, ydq_send, dkv_own, dkv_send, grad_ref, later_ref = rest[-6:]
    width = k_got.shape[1]
    own_at = [half_cols(core_ref[0], width, pair, head) for head in range(2)]
    got_at = [half_cols(0, width, pair, head) for head in range(2)]
    first_core = core_ref[0] == 0
    row, col = positions()
    causal = row <= col

    def mask(x):
        return jnp.where(causal, x, 0.0)

    def blocks(own, got):
        found = []
        for head in range(2):
            mine, other = own[:, own_at[head]], got[:, got_at[head]]
            found += [jnp.where(first_core, mine, other), jnp.where(first_core, other, mine)]
        return found

    k, v = blocks(k_ref, k_got), blocks(v_ref, v_got)
    q_t, g_t = each(jnp.transpose, blocks(q_ref, q_got)), each(jnp.transpose, blocks(g_ref, g_got))
    k_s, v_s = each(split, k), each(split, v)
    kt_s = each(lambda x: split(x.T), k)
    vt_s = each(lambda x: split(x.T), v)
    kk_prior, vk_prior = unpack(prior_ref, pair)
    damp, kk, vk = [], [], []
    for head in range(2):
        across = jnp.broadcast_to(damp_ref[0:1, own_at[head]], (DK, DK)).T
        damp += [across, across]
        early = 2 * head
        kk += [kk_prior[head], kk_prior[head] + mm(kt_s[early], k_s[early])]
        vk += [vk_prior[head], vk_prior[head] + mm(vt_s[early], k_s[early])]
    g_s = each(split, g_t)
    system = each(lambda s, kt: beside(split(s), kt), kk, kt_s)
    to_solved = each(lambda s, kt: beside(split(s.T), kt), vk, kt_s)
    to_out = each(lambda s, vt: beside(split(s), vt), vk, vt_s)

    def total(a, b):
        return jnp.sum(a * b, axis=0, keepdims=True)

    def apply(x):
        x_s = each(split, x)
        scores = each(lambda ks, xs: mask(mm(ks, xs)), k_s, x_s)
        scores_s = each(split, scores)
        image = each(lambda s, xs, ss, d, x1: mm(s, above(xs, ss)) + d * x1, system, x_s, scores_s, damp, x)
        return image, scores, x_s, scores_s

    y_scores_s = each(lambda vs, gs: split(mask(mm(vs, gs))), v_s, g_s)
    x_bar = each(lambda t, gs, ys: mm(t, above(gs, ys)), to_solved, g_s, y_scores_s)

    p0 = q_t
    rho0 = each(total, p0, p0)
    w0, d0, p0_s, d0_s = apply(p0)
    gam0 = each(total, p0, w0)
    al0 = each(lambda a, b: a / b, rho0, gam0)
    r1 = each(lambda p, a, w: p - a * w, p0, al0, w0)
    rho1 = each(total, r1, r1)
    be0 = each(lambda a, b: a / b, rho1, rho0)
    p1 = each(lambda r, b, p: r + b * p, r1, be0, p0)
    w1, d1, p1_s, d1_s = apply(p1)
    gam1 = each(total, p1, w1)
    al1 = each(lambda a, b: a / b, rho1, gam1)
    r2 = each(lambda r, a, w: r - a * w, r1, al1, w1)
    rho2 = each(total, r2, r2)
    be1 = each(lambda a, b: a / b, rho2, rho1)
    p2 = each(lambda r, b, p: r + b * p, r2, be1, p1)
    w2, d2, p2_s, d2_s = apply(p2)
    gam2 = each(total, p2, w2)
    al2 = each(lambda a, b: a / b, rho2, gam2)

    def mix(a0, x0, a1, x1, a2, x2):
        return a0 * x0 + a1 * x1 + a2 * x2

    x_s = each(lambda *a: split(mix(*a)), al0, p0, al1, p1, al2, p2)
    xs_s = each(lambda *a: split(mix(*a)), al0, d0, al1, d1, al2, d2)
    y_t = each(lambda t, xs, ss: mm(t, above(xs, ss)), to_out, x_s, xs_s)
    vk_grad = each(mm_t, g_s, x_s)
    v_grad = each(mm_t, xs_s, g_s)

    ab2 = each(total, x_bar, p2)
    gb2 = each(lambda a, l, g: -a * l / g, ab2, al2, gam2)
    pb2 = each(lambda l, x, g, w: l * x + (2.0 * g) * w, al2, x_bar, gb2, w2)
    bb1 = each(total, pb2, p1)
    rho2b = each(lambda a, g, b, r: a / g + b / r, ab2, gam2, bb1, rho1)
    rb2 = each(lambda p, b, r: p + (2.0 * b) * r, pb2, rho2b, r2)
    ab1 = each(lambda x, p, r, w: jnp.sum(x * p - r * w, axis=0, keepdims=True), x_bar, p1, rb2, w1)
    gb1 = each(lambda a, l, g: -a * l / g, ab1, al1, gam1)
    e2, _, rb2_s, s2_s = apply(rb2)
    pb1 = each(
        lambda l, x, b, p, g, w, e: l * (x - e) + b * p + (2.0 * g) * w, al1, x_bar, be1, pb2, gb1, w1, e2
    )
    bb0 = each(total, pb1, p0)
    rho1b = each(
        lambda b1, be, r1_, a, g, b0, r0: (a / g - b1 * be / r1_) + b0 / r0, bb1, be1, rho1, ab1, gam1, bb0, rho0
    )
    rb1 = each(lambda r, p, b, r1_: r + p + (2.0 * b) * r1_, rb2, pb1, rho1b, r1)
    ab0 = each(lambda x, p, r, w: jnp.sum(x * p - r * w, axis=0, keepdims=True), x_bar, p0, rb1, w0)
    gb0 = each(lambda a, l, g: -a * l / g, ab0, al0, gam0)
    e1, _, rb1_s, s1_s = apply(rb1)
    pb0 = each(
        lambda l, x, b, p, g, w, e: l * (x - e) + b * p + (2.0 * g) * w, al0, x_bar, be0, pb1, gb0, w0, e1
    )
    rho0b = each(lambda a, g, b, be, r: a / g - b * be / r, ab0, gam0, bb0, be0, rho0)
    q_grad = each(lambda p, r, b, q: p + r + (2.0 * b) * q, pb0, rb1, rho0b, p0)

    wb2 = each(lambda g, p: g * p, gb2, p2)
    wb1 = each(lambda g, p, a, r: g * p - a * r, gb1, p1, al1, rb2)
    wb0 = each(lambda g, p, a, r: g * p - a * r, gb0, p0, al0, rb1)
    kk_half = each(
        lambda a, b, c, x, y, z: mm_t(beside(split(a), split(b), split(c)), beside(x, y, z)),
        wb0, wb1, wb2, p0_s, p1_s, p2_s,
    )
    kk_grad = each(lambda x: x + x.T, kk_half)
    k_grad = each(
        lambda d2_, s2, d1_, s1, d0_, ys, b2, p2_, w1_, b1, p1_, a1, w0_, b0, p0_, a0, xs: mm_t(
            beside(d2_, s2, d1_, s1, d0_, ys),
            beside(
                split((2.0 * b2) * p2_), split(-a1 * p1_), split(w1_ + b1 * p1_),
                split(-a0 * p0_), split(w0_ + b0 * p0_), xs,
            ),
        ),
        d2_s, s2_s, d1_s, s1_s, d0_s, y_scores_s, gb2, p2, wb1, gb1, p1, al1, wb0, gb0, p0, al0, x_s,
    )

    y_grads = each(jnp.transpose, y_t), each(jnp.transpose, q_grad)
    for values, own, send in ((y_grads, ydq_own, ydq_send), ((k_grad, v_grad), dkv_own, dkv_send)):
        for at in range(2):
            for head in range(2):
                early, late = values[at][2 * head], values[at][2 * head + 1]
                own[at, :, got_at[head]] = jnp.where(first_core, early, late)
                send[at, :, got_at[head]] = jnp.where(first_core, late, early)
    kk_both, vk_both = ([x[0] + x[1], x[2] + x[3]] for x in (kk_grad, vk_grad))
    pack_into(grad_ref, pair, *kk_both, *vk_both)
    pack_into(later_ref, pair, kk_grad[1], kk_grad[3], vk_grad[1], vk_grad[3])


def slot_kernel(slot, chips, arrived, sent, turned, pairs, core_ref, chip_ref, *refs):
    refs = list(refs)
    count = {None: 0, "up": 1, "down": 1, "both": 2}
    came = [refs.pop(0)[0] for _ in range(count[arrived])]
    sums, grads, laters, _, _, prior_ref, after_ref = (refs.pop(0) for _ in range(7))
    chip = chip_ref[0]
    even = chip % 2 == 0
    up, down = slot - chip, slot - 2 * chips + 1 + chip
    up_at, down_at = jnp.clip(up, 0, pairs - 1), jnp.clip(down, 0, pairs - 1)
    if arrived in ("up", "both"):

        @pl.when((chip > 0) & (up >= 0) & (up < pairs))
        def _():
            prior_ref[up_at] = came[0] if arrived == "up" else jnp.where(even, came[1], came[0])

    if arrived in ("down", "both"):

        @pl.when((chip < chips - 1) & (down >= 0) & (down < pairs))
        def _():
            after_ref[down_at] = came[0] if arrived == "down" else jnp.where(even, came[0], came[1])

    going = [refs.pop(0) for _ in range(count[sent])]
    if sent in ("up", "both"):
        sent_up = prior_ref[up_at] + sums[up_at]
    if sent in ("down", "both"):
        sent_down = after_ref[down_at] + grads[down_at]
    if sent == "up":
        going[0][0] = sent_up
    if sent == "down":
        going[0][0] = sent_down
    if sent == "both":
        going[0][0] = jnp.where(even, sent_up, sent_down)
        going[1][0] = jnp.where(even, sent_down, sent_up)
    if turned is not None:
        own, other = refs.pop(0), refs.pop(0)
        second = after_ref[turned]
        first = second + laters[turned]
        first_core = core_ref[0] == 0
        own[0] = jnp.where(first_core, first, second)
        other[0] = jnp.where(first_core, second, first)


def final_kernel(pair, core_ref, chip_ref, k_ref, v_ref, dkv_own, dkv_got, after_own, after_got, *rest):
    dk_out, dv_out, dk_at, dv_at, sems = rest[-5:]
    width = dkv_got.shape[2]
    copies = []
    for at, (dkv_ref, after_ref) in enumerate(((dkv_own, after_own), (dkv_got, after_got))):
        half = core_ref[0] if at == 0 else 1 - core_ref[0]
        kk_after, vk_after = unpack(after_ref, 0)
        for head in range(2):
            cols, part, to = half_cols(half, width, pair, head), half_cols(0, width, pair, head), head_cols(head)
            k_s, v_s = split(k_ref[:, cols]), split(v_ref[:, cols])
            kk_s, vk_s = split(kk_after[head]), split(vk_after[head])
            dk_at[at, :, to] = dkv_ref[0, :, part] + mm(beside(k_s, v_s), above(kk_s, vk_s))
            dv_at[at, :, to] = dkv_ref[1, :, part] + mm_t(k_s, vk_s)
        cols = pl.ds(pl.multiple_of(pl.multiple_of(half * width, DK) + 2 * pair * DK, DK), 2 * DK)
        for which, (src, dst) in enumerate(((dk_at, dk_out), (dv_at, dv_out))):
            copies.append(pltpu.make_async_copy(src.at[at], dst.at[:, cols], sems.at[at, which]))
            copies[-1].start()
    for copy in copies:
        copy.wait()


def halves_kernel(core_ref, chip_ref, a_ref, b_ref, a_half, b_half, sems):
    width = a_half.shape[1]
    cols = pl.ds(pl.multiple_of((1 - core_ref[0]) * width, DK), width)
    copies = [
        pltpu.make_async_copy(src.at[:, cols], dst, sems.at[which])
        for which, (src, dst) in enumerate(((a_ref, a_half), (b_ref, b_half)))
    ]
    for copy in copies:
        copy.start()
    for copy in copies:
        copy.wait()


def place_kernel(core_ref, chip_ref, own_ref, got_ref, y_ref, dq_ref, sems):
    width = got_ref.shape[2]
    copies = []
    for which, (half, src) in enumerate(((core_ref[0], own_ref), (1 - core_ref[0], got_ref))):
        cols = pl.ds(pl.multiple_of(half * width, DK), width)
        for at, ref in enumerate((y_ref, dq_ref)):
            copies.append(pltpu.make_async_copy(src.at[at], ref.at[:, cols], sems.at[which, at]))
            copies[-1].start()
    for copy in copies:
        copy.wait()


ANYWHERE = pl.BlockSpec(memory_space=pl.ANY)
LOCAL = pl.BlockSpec(memory_space=pltpu.VMEM)
REMOTE = pl.BlockSpec(memory_space=pltpu.HBM)


def call(kernel, grid, args, in_specs, outs, out_specs, flops, aliases=None, scratch=()):
    return pl.pallas_call(
        kernel,
        grid_spec=pltpu.PrefetchScalarGridSpec(
            num_scalar_prefetch=2, grid=(grid,), in_specs=in_specs, out_specs=out_specs, scratch_shapes=scratch
        ),
        out_shape=[jax.ShapeDtypeStruct(shape, f32) for shape in outs],
        input_output_aliases=aliases or {},
        compiler_params=pltpu.CompilerParams(vmem_limit_bytes=VMEM_BYTES),
        cost_estimate=pl.CostEstimate(flops=COST, bytes_accessed=COST, transcendentals=0),
    )(*args)


def body(queries, key_vectors, value_vectors, damping, grad_output, sub_size):
    assert sub_size == 2 and queries.shape[0] == DK
    core = lax.axis_index("sub")
    chips = lax.axis_size("ctx")
    whole = queries.shape[1]
    width = whole // 2
    pairs = width // (2 * DK)
    swap = [(0, 1), (1, 0)]
    at = tuple(lax.axis_index(name).astype(jnp.int32).reshape(1) for name in ("sub", "ctx"))
    unit = 2 * DK**3

    state_shape, states_shape = (1, ROWS, DK), (pairs, ROWS, DK)
    damp_row = damping.reshape(1, -1)

    def exchanges(slot, sent):
        ups = [(a, a + 1) for a in range(chips - 1) if 0 <= slot - a < pairs]
        downs = [(b, b - 1) for b in range(1, chips) if 0 <= slot - 2 * chips + 1 + b < pairs]
        if sent == "both":
            near = [(a, a ^ 1 if a ^ 1 < chips else a) for a in range(chips)]
            far = [(a, b if 0 <= b < chips else a) for a in range(chips) for b in [a - 1 if a % 2 == 0 else a + 1]]
            return [near, far]
        links = ups if sent == "up" else downs
        if len(links) < 2 or chips < 3:
            return [links]
        step = 1 if sent == "up" else -1
        return [[(a, (a + step) % chips) for a in range(chips)]]

    done = []

    def after(x):
        return lax.optimization_barrier((x, *done))[0] if done else x

    def mark(x):
        done[:] = [x]
        return x

    def swapped(a, b):
        halves = call(
            halves_kernel, 1, (*at, a, b), [REMOTE] * 2, [(DK, width)] * 2, [LOCAL] * 2, 1,
            scratch=[pltpu.SemaphoreType.DMA((2,))],
        )
        return [lax.ppermute(after(x), "sub", swap) for x in halves]


    mine = pl.BlockSpec((DK, 2 * DK), lambda i, core_at, chip_at: (0, core_at[0] * pairs))
    theirs = pl.BlockSpec((DK, 2 * DK), lambda i, core_at, chip_at: (0, (1 - core_at[0]) * pairs))
    first_own, first_other = call(
        first_kernel, 1, (*at, key_vectors, value_vectors, key_vectors, value_vectors), [mine, mine, theirs, theirs],
        [state_shape] * 2, [LOCAL] * 2, 1,
    )
    first_got = lax.ppermute(first_other, "sub", swap)
    sums, prior, later_sums = call(
        start_kernel, 1, (*at, first_own, first_got), [LOCAL] * 2, [states_shape] * 3, [LOCAL] * 3, 1
    )
    mark(sums)
    grad, later = later_sums, later_sums
    bulk, grads, arrived, waiting = (), (), None, []
    came = ()

    def run_final(pair, after_own, after_got):
        nonlocal grads
        grads = call(
            functools.partial(final_kernel, pair), 1,
            (*at, key_vectors, value_vectors, bulk[2], dkv_got, after(after_own), after_got, *grads),
            [LOCAL] * 6 + [ANYWHERE] * len(grads), [(DK, whole)] * 2, [ANYWHERE] * 2, 1,
            aliases={8: 0, 9: 1} if grads else None,
            scratch=[pltpu.VMEM((2, DK, 2 * DK), f32)] * 2 + [pltpu.SemaphoreType.DMA((2, 2))],
        )
        mark(grads[0])

    last_up, last_down = pairs + chips - 3, pairs + 2 * chips - 3
    for slot in range(last_down + 2):
        up, down = slot <= last_up, chips <= slot <= last_down
        sent = "both" if up and (down or slot >= chips - 2) else "up" if up else "down" if down else None
        turned = slot - 2 * chips + 1
        turned = turned if 0 <= turned < pairs else None
        ways = {None: 0, "both": 2}.get(sent, 1)
        extra = ways + 2 * (turned is not None)
        n = len(came)
        outs = call(
            functools.partial(slot_kernel, slot, chips, arrived, sent, turned, pairs), 1,
            (*at, *came, sums, grad, later, prior, after(later_sums)),
            [LOCAL] * (n + 5), [states_shape] * 2 + [state_shape] * extra, [LOCAL] * (2 + extra), 1,
            aliases={n + 5: 0, n + 6: 1},
        )
        prior, later_sums, *outs = outs
        mark(prior)
        came = [lax.ppermute(outs.pop(0), "ctx", pairing) for pairing in (exchanges(slot, sent) if sent else ())]
        arrived = sent
        if turned is not None:
            waiting.append((turned, outs[0], lax.ppermute(outs[1], "sub", swap)))
        if slot == last_down:
            y, dq = call(
                place_kernel, 1, (*at, bulk[0], after(ydq_got)), [LOCAL] * 2, [(DK, whole)] * 2, [ANYWHERE] * 2, 1,
                scratch=[pltpu.SemaphoreType.DMA((2, 2))],
            )
            mark(y)
        while waiting and (slot > last_down or (slot == last_down and len(waiting) > 1)):
            run_final(*waiting.pop(0))
        if slot == 0:
            k_got, v_got = swapped(key_vectors, value_vectors)
            kv = key_vectors, value_vectors, k_got, v_got
        if slot == 0 and pairs > 1:
            (sums,) = call(
                functools.partial(sums_kernel, 1, pairs), 1, (*at, *kv, after(sums)), [LOCAL] * 5, [states_shape], [LOCAL], 1,
                aliases={6: 0},
            )
            mark(sums)
        if slot == 1:
            q_got, g_got = swapped(queries, grad_output)
        pair = slot - chips + 1
        if 0 <= pair < pairs:
            carried = (*bulk, grad, later) if bulk else ()
            outs = call(
                functools.partial(main_kernel, pair), 1,
                (*at, queries, key_vectors, value_vectors, grad_output, q_got, k_got, v_got, g_got, damp_row, after(prior), *carried),
                [LOCAL] * (10 + len(carried)), [(2, DK, width)] * 4 + [states_shape] * 2, [LOCAL] * 6, 1,
                aliases={12 + k: k for k in range(6)} if carried else None,
            )
            *bulk, grad, later = outs
            mark(grad)
        if slot == last_down - 1:
            dkv_got = lax.ppermute(after(bulk[3]), "sub", swap)
            ydq_got = lax.ppermute(after(bulk[1]), "sub", swap)
    return (y, dq, *grads)


def solution(mesh):
    split_both = P(("groups", "ctx", "sub"), "head")
    return jax.shard_map(
        functools.partial(body, sub_size=mesh.shape["sub"]),
        mesh=mesh,
        in_specs=(split_both, split_both, split_both, P("head"), split_both),
        out_specs=(split_both,) * 4,
        check_vma=False,
    )
```
